32 devices in a mesh: groups: 2 (over y), ctx: 4 (over z), dp: 4 (over x, core).
Axes of the slice: x: 2, y: 2, z: 4, core: 2. Of those that a mesh axis runs over, the one named last changes fastest.
Arguments:
- queries: bfloat16 [8, 512, 2048], P(('groups', 'dp'), 'ctx'), parts along dimension 0, may hold values from -10 to 10
- keys: bfloat16 [8, 512, 2048], P(('groups', 'dp'), 'ctx'), parts along dimension 0, may hold values from -10 to 10
- values: bfloat16 [8, 512, 2048], P(('groups', 'dp'), 'ctx'), parts along dimension 0, may hold values from -6 to 6
- grad_out: bfloat16 [8, 512, 2048], P(('groups', 'dp'), 'ctx'), parts along dimension 0, may hold values from -6 to 6
- rand_blocks: int32 [8, 8, 3], P(('groups', 'dp')), parts along dimension 0, may hold values from 0 to 7, as said below
- glob_blocks: int32 [8, 2], P(('groups', 'dp')), parts along dimension 0, may hold values from 0 to 7, as said below
Outputs:
- attn_out: bfloat16 [8, 512, 2048], P(('groups', 'dp'), 'ctx'), parts along dimension 0
- grad_queries: bfloat16 [8, 512, 2048], P(('groups', 'dp'), 'ctx'), parts along dimension 0
- grad_keys: bfloat16 [8, 512, 2048], P(('groups', 'dp'), 'ctx'), parts along dimension 0
- grad_values: bfloat16 [8, 512, 2048], P(('groups', 'dp'), 'ctx'), parts along dimension 0
The draws below stay inside these ranges and needn't reach their ends.
There are 2 independent parts, one for each index of `groups`. The reference program is written for one: setup_inputs(seed, part) draws one part's arguments, and reference() takes and returns one part's arrays. A program takes and returns all parts, laid end to end along the dimension named above; each array names one. Nothing has to cross between parts.
Inputs may be any that keep to these rules, and one draw needn't show every extreme that they name: `rand_blocks`: block b lies on index b // 2 of ctx. The 3 random blocks of one query block lie on 3 different indices of ctx, none on the index that holds the query block. The query blocks of one index of ctx name at most 2 random blocks on any one other index, and exactly 2 on some index. `glob_blocks`: the 2 global blocks of a sequence are distinct.
All inputs are finite; a program needn't handle non-finite values.
Results may differ from the reference program's by a relative error of at most 0.013.
Values may be sent and summed in bfloat16 or wider, within the bound.
No kernel may reach another device: no remote copies, remote signals or barrier semaphores. Data moves between devices by JAX's collectives and lax.ppermute only.
A program may use at most 128 MiB of HBM per device.

```python
import jax
import jax.numpy as jnp
from jax import lax

HEADS = 16
HEAD_DIM = 128
BLOCK = 64
GLOBALS = 2
RAND = 3
TOK_DEV = 128
WIDTH = 2048
SEQS = 4
LENGTH = 512
NQB = 8
N_CTX = 4


def draw_queries(key, part):
    result = 1.5 * jax.random.truncated_normal(jax.random.fold_in(key, 31), -6.0, 6.0, (SEQS, LENGTH, HEADS * HEAD_DIM))
    return result.astype(jnp.float32).astype(jnp.bfloat16)


def draw_keys(key, part):
    result = 1.5 * jax.random.truncated_normal(jax.random.fold_in(key, 32), -6.0, 6.0, (SEQS, LENGTH, HEADS * HEAD_DIM))
    return result.astype(jnp.float32).astype(jnp.bfloat16)


def draw_rand_blocks(key, part):
    local_count = TOK_DEV // BLOCK
    slot_count = local_count * RAND
    others = N_CTX - 1
    row_keys = jax.random.split(jax.random.fold_in(key, 41), SEQS * N_CTX)
    orders = jax.vmap(lambda row_key: jax.random.permutation(row_key, others))(row_keys)
    picked = jnp.take(orders, jnp.arange(slot_count) % others, axis=1)
    devices = jnp.arange(SEQS * N_CTX, dtype=jnp.int32) % N_CTX
    holders = (devices[:, None] + 1 + picked) % N_CTX
    local_rows = jax.random.randint(jax.random.fold_in(key, 42), (SEQS * N_CTX, slot_count), 0, local_count)
    blocks = holders * local_count + local_rows
    return blocks.reshape(SEQS, N_CTX * local_count, RAND).astype(jnp.int32)


def draw_glob_blocks(key, part):
    row_keys = jax.random.split(jax.random.fold_in(key, 51), SEQS)
    chosen = jax.vmap(lambda row_key: jax.random.permutation(row_key, NQB)[:GLOBALS])(row_keys)
    return chosen.astype(jnp.int32)


def shard_levels(key, extent, cuts, smallest, top_value):
    gain, own = 1.0, jax.random.fold_in(key, 6)
    for dim, blocks in cuts:
        steps = jnp.exp(jax.random.uniform(jax.random.fold_in(own, dim), (blocks,), jnp.float32, smallest / len(cuts), top_value / len(cuts)))
        gain = gain * jnp.repeat(steps, extent[dim] // blocks).reshape([-1 if axis == dim else 1 for axis in range(len(extent))])
    return gain


def centred(own_key, shape, width, bound, pieces=(), kind=jnp.bfloat16):
    loudness = shard_levels(own_key, shape, pieces, -0.22, 0.18) if pieces else 1.0
    drawn = jax.random.normal(own_key, shape, jnp.float32) * width * loudness
    return jnp.minimum(jnp.maximum(drawn, -bound), bound).astype(kind)


def setup_inputs(seed: int = 0, part: int = 0) -> dict:
    splits = jax.random.split(jax.random.key(seed), 7)
    part_keys = jax.random.split(jax.random.fold_in(splits[6], part), 7)
    return {
        "queries": draw_queries(jax.random.fold_in(jax.random.fold_in(splits[6], part), 71), part),
        "keys": draw_keys(jax.random.fold_in(jax.random.fold_in(splits[6], part), 71), part),
        "values": centred(part_keys[2], (SEQS, LENGTH, WIDTH), 1.0, 6.0, ((0, 4), (1, 4))),
        "grad_out": centred(part_keys[3], (SEQS, LENGTH, WIDTH), 1.0, 6.0, ((0, 4), (1, 4))),
        "rand_blocks": draw_rand_blocks(jax.random.fold_in(jax.random.fold_in(splits[6], part), 71), part),
        "glob_blocks": draw_glob_blocks(jax.random.fold_in(jax.random.fold_in(splits[6], part), 71), part),
    }


def sequence_pass(packed):
    queries, keys, values, grad_out, rand_rows, global_ids = packed
    total_blocks = LENGTH // BLOCK
    feature_width = queries.shape[1]
    head_dim = feature_width // HEADS
    score_scale = head_dim ** -0.5
    query_blocks = queries.reshape(total_blocks, BLOCK, HEADS, head_dim)
    key_blocks = keys.reshape(total_blocks, BLOCK, HEADS, head_dim)
    value_blocks = values.reshape(total_blocks, BLOCK, HEADS, head_dim)
    grad_blocks = grad_out.reshape(total_blocks, BLOCK, HEADS, head_dim)

    def one_block(carry, block_index):
        grad_k, grad_v = carry
        window_ids = jnp.stack([(block_index - 1) % total_blocks, block_index, (block_index + 1) % total_blocks]).astype(jnp.int32)
        random_ids = rand_rows[block_index].astype(jnp.int32)
        block_list = jnp.concatenate([global_ids.astype(jnp.int32), window_ids, random_ids])
        window_ok = ~jnp.any(window_ids[:, None] == global_ids[None, :], axis=1)
        random_ok = ~(jnp.any(random_ids[:, None] == global_ids[None, :], axis=1) | jnp.any(random_ids[:, None] == window_ids[None, :], axis=1))
        block_ok = jnp.concatenate([jnp.ones((global_ids.shape[0],), dtype=bool), window_ok, random_ok])
        valid = jnp.repeat(block_ok, BLOCK)
        key_rows = key_blocks[block_list].reshape(-1, HEADS, head_dim)
        value_rows = value_blocks[block_list].reshape(-1, HEADS, head_dim)
        query = query_blocks[block_index]
        grad_rows = grad_blocks[block_index]
        scores = jnp.einsum("qhd,khd->hqk", query.astype(jnp.float32), key_rows.astype(jnp.float32)) * score_scale
        scores = jnp.where(valid[None, None, :], scores, -jnp.inf)
        top = jnp.max(scores, axis=2, keepdims=True)
        expo = jnp.exp(scores - top)
        prob = expo / jnp.sum(expo, axis=2, keepdims=True)
        prob_b = prob.astype(jnp.bfloat16)
        attended = jnp.einsum("hqk,khd->qhd", prob_b.astype(jnp.float32), value_rows.astype(jnp.float32))
        out_block = attended.astype(jnp.bfloat16)
        delta = jnp.sum(grad_rows.astype(jnp.float32) * out_block.astype(jnp.float32), axis=2)
        dprob = jnp.einsum("qhd,khd->hqk", grad_rows.astype(jnp.float32), value_rows.astype(jnp.float32))
        dscore = prob * (dprob - jnp.transpose(delta)[:, :, None])
        dscore_b = dscore.astype(jnp.bfloat16)
        dquery = jnp.einsum("hqk,khd->qhd", dscore_b.astype(jnp.float32), key_rows.astype(jnp.float32)) * score_scale
        dkey = jnp.einsum("hqk,qhd->khd", dscore_b.astype(jnp.float32), query.astype(jnp.float32)) * score_scale
        dvalue = jnp.einsum("hqk,qhd->khd", prob_b.astype(jnp.float32), grad_rows.astype(jnp.float32))
        grad_k = grad_k.at[block_list].add(dkey.reshape(-1, BLOCK, feature_width))
        grad_v = grad_v.at[block_list].add(dvalue.reshape(-1, BLOCK, feature_width))
        return (grad_k, grad_v), (out_block.reshape(BLOCK, feature_width), dquery.astype(jnp.bfloat16).reshape(BLOCK, feature_width))

    zeros = jnp.zeros((total_blocks, BLOCK, feature_width), jnp.float32)
    (grad_k, grad_v), (outs, dqs) = lax.scan(one_block, (zeros, zeros), jnp.arange(total_blocks, dtype=jnp.int32))
    return (outs.reshape(LENGTH, feature_width), dqs.reshape(LENGTH, feature_width),
            grad_k.astype(jnp.bfloat16).reshape(LENGTH, feature_width),
            grad_v.astype(jnp.bfloat16).reshape(LENGTH, feature_width))


def reference(queries, keys, values, grad_out, rand_blocks, glob_blocks):
    attn_out, grad_queries, grad_keys, grad_values = lax.map(sequence_pass, (queries, keys, values, grad_out, rand_blocks, glob_blocks))
    return (attn_out, grad_queries, grad_keys, grad_values)
```

```python
import functools

import jax
import jax.numpy as jnp
from jax import lax
from jax.experimental import pallas as pl
from jax.experimental.pallas import tpu as pltpu
from jax.sharding import PartitionSpec as P

HEADS = 16
BLOCK = 64
QUERY_TILE = 512
ANY = pl.BlockSpec(memory_space=pl.ANY)


def pack_kernel(me_ref, *refs, ranks, width):
    arrays, outs, sems = refs[:4], refs[4 : 4 + ranks - 1], refs[-1]
    copies = []
    for shift in range(1, ranks):
        start = pl.multiple_of(lax.rem(me_ref[0] + shift, ranks) * width, 128)
        for i, array in enumerate(arrays):
            copies.append(
                pltpu.make_async_copy(
                    array.at[:, pl.ds(start, width)],
                    outs[shift - 1].at[i],
                    sems.at[shift - 1, i],
                )
            )
    for copy in copies:
        copy.start()
    for copy in copies:
        copy.wait()


def unpack_kernel(me_ref, *refs, ranks, width):
    pieces, outs, sems = refs[4 : 4 + ranks - 1], refs[4 + ranks - 1 : -1], refs[-1]
    copies = []
    for shift in range(1, ranks):
        start = pl.multiple_of(lax.rem(me_ref[0] + shift, ranks) * width, 128)
        for i, out in enumerate(outs):
            copies.append(
                pltpu.make_async_copy(
                    pieces[shift - 1].at[i],
                    out.at[:, pl.ds(start, width)],
                    sems.at[shift - 1, i],
                )
            )
    for copy in copies:
        copy.start()
    for copy in copies:
        copy.wait()


def attention_kernel(me_ref, bias_ref, *refs, ranks, tokens, scale):
    own, got = refs[:4], refs[4 : 4 + ranks - 1]
    own_outs, sent = refs[3 + ranks : 7 + ranks], refs[7 + ranks :]
    f32, bf16 = jnp.float32, jnp.bfloat16
    length = ranks * tokens
    tile = min(QUERY_TILE, length)

    def whole(i):
        return jnp.concatenate([own[i][...]] + [piece[i] for piece in got], axis=0)

    def dot(a, b):
        return jnp.dot(a, b, preferred_element_type=f32)

    def give(i, first, value):
        for r in range(value.shape[0] // tokens):
            rank, part = first // tokens + r, value[r * tokens : (r + 1) * tokens]
            if rank == 0:
                own_outs[i][...] = part
            else:
                sent[rank - 1][i] = part

    query, key, val, dout = (whole(i) for i in range(4))
    key_t, val_t = key.T, val.T
    dkey = dval = None
    for first in range(0, length, tile):
        q = query[first : first + tile]
        g = dout[first : first + tile]
        g_t = g.T
        scores = dot(key, q.T).reshape(-1, BLOCK, tile)
        bias = bias_ref[:, first : first + tile]
        scores = (scores + bias[:, None, :]).reshape(length, tile)
        top = jnp.max(scores, axis=0, keepdims=True)
        expo = jnp.exp((scores - top) * scale)
        prob = expo * (1.0 / jnp.sum(expo, axis=0, keepdims=True))
        prob_b = prob.astype(bf16)
        out_t = dot(val_t, prob_b).astype(bf16)
        delta = jnp.sum(g_t.astype(f32) * out_t.astype(f32), axis=0, keepdims=True)
        dscore = (prob * (dot(val, g_t) - delta)).astype(bf16)
        dquery_t = (dot(key_t, dscore) * scale).astype(bf16)
        give(0, first, out_t.T)
        give(1, first, dquery_t.T)
        dk, dv = dot(dscore, q), dot(prob_b, g)
        dkey = dk if dkey is None else dkey + dk
        dval = dv if dval is None else dval + dv
    give(2, 0, (dkey * scale).astype(bf16))
    give(3, 0, dval.astype(bf16))


def block_bias(rand_blocks, glob_blocks, me, ranks, local_blocks):
    total = ranks * local_blocks
    ids = jnp.arange(total, dtype=jnp.int32)
    order = (me - ids // local_blocks) % ranks * local_blocks + ids % local_blocks
    rand = jnp.take(rand_blocks, order, axis=0)
    gap = (order[:, None] - order[None, :]) % total
    near = (gap <= 1) | (gap == total - 1)
    glob = jnp.any(order[:, None] == glob_blocks[None, :], axis=1)
    picked = jnp.any(order[:, None, None] == rand[None, :, :], axis=2)
    allowed = near | glob[:, None] | picked
    bias = jnp.where(allowed, 0.0, -jnp.inf).astype(jnp.float32)
    return jnp.repeat(bias, BLOCK, axis=1)


def local(queries, keys, values, grad_out, rand_blocks, glob_blocks):
    ranks = lax.axis_size("ctx")
    me = lax.axis_index("ctx")
    tokens, features = queries.shape[1], queries.shape[2]
    head_dim = features // HEADS
    heads = HEADS // ranks
    width = heads * head_dim
    bf16 = jnp.bfloat16
    me_arr = jnp.reshape(me, (1,)).astype(jnp.int32)
    arrays = [queries[0], keys[0], values[0], grad_out[0]]
    piece = jax.ShapeDtypeStruct((4, tokens, width), bf16)
    full = jax.ShapeDtypeStruct((tokens, features), bf16)
    smem = pl.BlockSpec(memory_space=pltpu.SMEM)
    sems = pltpu.SemaphoreType.DMA((ranks - 1, 4))

    outgoing = pl.pallas_call(
        functools.partial(pack_kernel, ranks=ranks, width=width),
        out_shape=[piece] * (ranks - 1),
        in_specs=[smem] + [ANY] * 4,
        out_specs=[ANY] * (ranks - 1),
        scratch_shapes=[sems],
    )(me_arr, *arrays)
    got = [
        lax.ppermute(x, "ctx", [(j, (j + s) % ranks) for j in range(ranks)])
        for s, x in enumerate(outgoing, 1)
    ]
    bias = block_bias(rand_blocks[0], glob_blocks[0], me, ranks, tokens // BLOCK)
    mine = pl.BlockSpec((tokens, head_dim), lambda h, m: (0, m[0] * heads + h))
    block = pl.BlockSpec((4, tokens, head_dim), lambda h, m: (0, 0, h))
    results = pl.pallas_call(
        functools.partial(
            attention_kernel, ranks=ranks, tokens=tokens, scale=head_dim ** (-0.5)
        ),
        out_shape=[full] * 4 + [piece] * (ranks - 1),
        grid_spec=pltpu.PrefetchScalarGridSpec(
            num_scalar_prefetch=1,
            grid=(heads,),
            in_specs=[pl.BlockSpec(bias.shape, lambda h, m: (0, 0))]
            + [mine] * 4
            + [block] * (ranks - 1),
            out_specs=[mine] * 4 + [block] * (ranks - 1),
        ),
        compiler_params=pltpu.CompilerParams(vmem_limit_bytes=56 << 20),
    )(me_arr, bias, *arrays, *got)
    partial, sent = results[:4], results[4:]
    back = [
        lax.ppermute(x, "ctx", [(j, (j - s) % ranks) for j in range(ranks)])
        for s, x in enumerate(sent, 1)
    ]
    outs = pl.pallas_call(
        functools.partial(unpack_kernel, ranks=ranks, width=width),
        out_shape=[full] * 4,
        in_specs=[smem] + [ANY] * (4 + ranks - 1),
        out_specs=[ANY] * 4,
        scratch_shapes=[sems],
        input_output_aliases={1 + i: i for i in range(4)},
    )(me_arr, *partial, *back)
    return tuple(x[None] for x in outs)


def solution(mesh):
    wide = P(("groups", "dp"), "ctx", None)
    return jax.shard_map(
        local,
        mesh=mesh,
        in_specs=(wide,) * 4 + (P(("groups", "dp"), None, None), P(("groups", "dp"), None)),
        out_specs=(wide,) * 4,
        check_vma=False,
    )
```

```python
import functools
import math

import jax
import jax.numpy as jnp
from jax import lax
from jax.experimental import pallas as pl
from jax.experimental.pallas import tpu as pltpu
from jax.sharding import PartitionSpec as P

HEADS = 16
BLOCK = 64
QUERY_TILE = 512
CHUNKS = 2
ANY = pl.BlockSpec(memory_space=pl.ANY)
SMEM = pl.BlockSpec(memory_space=pltpu.SMEM)
PARAMS = pltpu.CompilerParams(vmem_limit_bytes=56 << 20)


def pack_kernel(me_ref, *refs, ranks, chunks):
    arrays, outs = refs[:4], refs[4:]
    width = outs[0].shape[2]
    for chunk in range(chunks):
        for shift in range(1, ranks):
            dest = lax.rem(me_ref[0] + shift, ranks)
            start = pl.multiple_of((dest * chunks + chunk) * width, 128)
            out = outs[chunk * (ranks - 1) + shift - 1]
            for i, array in enumerate(arrays):
                out[i] = array[:, pl.ds(start, width)]


def unpack_kernel(me_ref, *refs, ranks):
    pieces, outs = refs[4 : 3 + ranks], refs[3 + ranks :]
    for shift in range(1, ranks):

        @pl.when(pl.program_id(0) == shift - 1)
        def _():
            for i, out in enumerate(outs):
                out[...] = pieces[shift - 1][i]


def attention_kernel(me_ref, bias_ref, *refs, ranks, tokens, scale):
    own, got = refs[:4], refs[4 : 3 + ranks]
    own_outs, sent = refs[-3 - ranks : 1 - ranks], refs[1 - ranks :]
    f32, bf16 = jnp.float32, jnp.bfloat16
    length = ranks * tokens
    tile = min(QUERY_TILE, length)

    def whole(i):
        return jnp.concatenate([own[i][...]] + [piece[i] for piece in got], axis=0)

    def dot(a, b):
        return jnp.dot(a, b, preferred_element_type=f32)

    def give(i, first, value):
        for r in range(value.shape[0] // tokens):
            rank, part = first // tokens + r, value[r * tokens : (r + 1) * tokens]
            if rank == 0:
                own_outs[i][...] = part
            else:
                sent[rank - 1][i] = part

    query, key, val, dout = (whole(i) for i in range(4))
    key_t, val_t = key.T, val.T
    dkey = dval = None
    for first in range(0, length, tile):
        q = query[first : first + tile]
        g = dout[first : first + tile]
        g_t = g.T
        scores = dot(key, q.T).reshape(-1, BLOCK, tile)
        bias = bias_ref[:, first : first + tile]
        scores = (scores + bias[:, None, :]).reshape(length, tile)
        top = jnp.max(scores, axis=0, keepdims=True)
        expo = jnp.exp((scores - top) * scale)
        prob = expo * (1.0 / jnp.sum(expo, axis=0, keepdims=True))
        prob_b = prob.astype(bf16)
        out_t = dot(val_t, prob_b).astype(bf16)
        delta = jnp.sum(g_t.astype(f32) * out_t.astype(f32), axis=0, keepdims=True)
        dscore = (prob * (dot(val, g_t) - delta)).astype(bf16)
        dquery_t = (dot(key_t, dscore) * scale).astype(bf16)
        give(0, first, out_t.T)
        give(1, first, dquery_t.T)
        dk, dv = dot(dscore, q), dot(prob_b, g)
        dkey = dk if dkey is None else dkey + dk
        dval = dv if dval is None else dval + dv
    give(2, 0, (dkey * scale).astype(bf16))
    give(3, 0, dval.astype(bf16))


def block_bias(rand_blocks, glob_blocks, me, ranks, local_blocks):
    total = ranks * local_blocks
    ids = jnp.arange(total, dtype=jnp.int32)
    order = (me - ids // local_blocks) % ranks * local_blocks + ids % local_blocks
    rand = jnp.take(rand_blocks, order, axis=0)
    gap = (order[:, None] - order[None, :]) % total
    near = (gap <= 1) | (gap == total - 1)
    glob = jnp.any(order[:, None] == glob_blocks[None, :], axis=1)
    picked = jnp.any(order[:, None, None] == rand[None, :, :], axis=2)
    allowed = near | glob[:, None] | picked
    bias = jnp.where(allowed, 0.0, -jnp.inf).astype(jnp.float32)
    return jnp.repeat(bias, BLOCK, axis=1)


def local(queries, keys, values, grad_out, rand_blocks, glob_blocks):
    ranks = lax.axis_size("ctx")
    me = lax.axis_index("ctx")
    tokens, features = queries.shape[1], queries.shape[2]
    head_dim = features // HEADS
    chunks = math.gcd(HEADS // ranks, CHUNKS)
    heads = HEADS // ranks // chunks
    width = heads * head_dim
    me_arr = jnp.reshape(me, (1,)).astype(jnp.int32)
    arrays = [queries[0], keys[0], values[0], grad_out[0]]
    piece = jax.ShapeDtypeStruct((4, tokens, width), jnp.bfloat16)
    full = jax.ShapeDtypeStruct((tokens, features), jnp.bfloat16)
    block = pl.BlockSpec((4, tokens, head_dim), lambda h, m: (0, 0, h))

    def attend(chunk, got, partial):
        first = chunk * heads
        mine = pl.BlockSpec(
            (tokens, head_dim), lambda h, m: (0, m[0] * (heads * chunks) + first + h)
        )
        results = pl.pallas_call(
            functools.partial(
                attention_kernel, ranks=ranks, tokens=tokens, scale=head_dim ** (-0.5)
            ),
            out_shape=[full] * 4 + [piece] * (ranks - 1),
            grid_spec=pltpu.PrefetchScalarGridSpec(
                num_scalar_prefetch=1,
                grid=(heads,),
                in_specs=[pl.BlockSpec(bias.shape, lambda h, m: (0, 0))]
                + [mine] * 4
                + [block] * (ranks - 1)
                + [ANY] * len(partial),
                out_specs=[mine] * 4 + [block] * (ranks - 1),
            ),
            input_output_aliases={5 + ranks + i: i for i in range(len(partial))},
            compiler_params=PARAMS,
        )(me_arr, bias, *arrays, *got, *partial)
        return results[:4], results[4:]

    def unpack(chunk, back, partial):
        whole = pl.BlockSpec((4, tokens, width), lambda s, m: (0, 0, 0))
        there = pl.BlockSpec(
            (tokens, width), lambda s, m: (0, lax.rem(m[0] + s + 1, ranks) * chunks + chunk)
        )
        return pl.pallas_call(
            functools.partial(unpack_kernel, ranks=ranks),
            out_shape=[full] * 4,
            grid_spec=pltpu.PrefetchScalarGridSpec(
                num_scalar_prefetch=1,
                grid=(ranks - 1,),
                in_specs=[ANY] * 4 + [whole] * (ranks - 1),
                out_specs=[there] * 4,
            ),
            input_output_aliases={1 + i: i for i in range(4)},
            compiler_params=PARAMS,
        )(me_arr, *partial, *back)

    outgoing = pl.pallas_call(
        functools.partial(pack_kernel, ranks=ranks, chunks=chunks),
        out_shape=[piece] * (chunks * (ranks - 1)),
        in_specs=[SMEM] + [pl.BlockSpec(memory_space=pltpu.VMEM)] * 4,
        compiler_params=PARAMS,
    )(me_arr, *arrays)
    got = [
        lax.ppermute(x, "ctx", [(j, (j + i % (ranks - 1) + 1) % ranks) for j in range(ranks)])
        for i, x in enumerate(outgoing)
    ]
    bias = block_bias(rand_blocks[0], glob_blocks[0], me, ranks, tokens // BLOCK)
    partial, back = [], []
    for chunk in range(chunks):
        partial, sent = attend(
            chunk, got[chunk * (ranks - 1) : (chunk + 1) * (ranks - 1)], partial
        )
        back.append(
            [
                lax.ppermute(x, "ctx", [(j, (j - s) % ranks) for j in range(ranks)])
                for s, x in enumerate(sent, 1)
            ]
        )
    for chunk in range(chunks):
        partial = unpack(chunk, back[chunk], partial)
    return tuple(x[None] for x in partial)


def solution(mesh):
    wide = P(("groups", "dp"), "ctx", None)
    return jax.shard_map(
        local,
        mesh=mesh,
        in_specs=(wide,) * 4 + (P(("groups", "dp"), None, None), P(("groups", "dp"), None)),
        out_specs=(wide,) * 4,
        check_vma=False,
    )
```

```python
import functools

import jax
import jax.numpy as jnp
from jax import lax
from jax.experimental import pallas as pl
from jax.experimental.pallas import tpu as pltpu
from jax.sharding import PartitionSpec as P

HEADS = 16
BLOCK = 64
QUERY_TILE = 512
ANY = pl.BlockSpec(memory_space=pl.ANY)
SMEM = pl.BlockSpec(memory_space=pltpu.SMEM)
VMEM = pl.BlockSpec(memory_space=pltpu.VMEM)
PARAMS = pltpu.CompilerParams(vmem_limit_bytes=48 << 20)


def pack_kernel(me_ref, *refs, ranks, wanted):
    arrays, outs, sems = refs[:4], refs[4:-1], refs[-1]
    features, width = arrays[0].shape[1], outs[0].shape[2]
    copies = []
    for n, (head, step) in enumerate(wanted):
        dest = me_ref[0] ^ step
        start = pl.multiple_of(dest * (features // ranks) + head * width, 128)
        for i, array in enumerate(arrays):
            copies.append(
                pltpu.make_async_copy(
                    array.at[:, pl.ds(start, width)], outs[n].at[i], sems.at[n, i]
                )
            )
    for copy in copies:
        copy.start()
    for copy in copies:
        copy.wait()


def unpack_kernel(me_ref, *refs, ranks, heads):
    pieces, outs, buffers, sems = refs[: ranks * heads], refs[ranks * heads : -2], refs[-2], refs[-1]
    features, width = outs[0].shape[1], pieces[0].shape[2]
    copies = []
    for i, out in enumerate(outs):
        for head in range(heads):
            for step in range(ranks):
                dest = me_ref[0] ^ step
                start = pl.multiple_of(dest * (features // ranks) + head * width, 128)
                buffers[i, :, pl.ds(start, width)] = pieces[head * ranks + step][i]
        copies.append(pltpu.make_async_copy(buffers.at[i], out, sems.at[i]))
        copies[-1].start()
    for copy in copies:
        copy.wait()


def attention_kernel(bias_ref, *refs, ranks, tokens, scale):
    got, sent = refs[:ranks], refs[ranks:]
    f32, bf16 = jnp.float32, jnp.bfloat16
    length = ranks * tokens
    tile = min(QUERY_TILE, length)

    def whole(i):
        return jnp.concatenate([piece[i] for piece in got], axis=0)

    def dot(a, b):
        return jnp.dot(a, b, preferred_element_type=f32)

    def give(i, first, value):
        for r in range(value.shape[0] // tokens):
            sent[first // tokens + r][i] = value[r * tokens : (r + 1) * tokens]

    query, key, val, dout = (whole(i) for i in range(4))
    key_t, val_t = key.T, val.T
    dkey = dval = None
    for first in range(0, length, tile):
        q = query[first : first + tile]
        g = dout[first : first + tile]
        g_t = g.T
        scores = dot(key, q.T).reshape(-1, BLOCK, tile)
        bias = bias_ref[:, first : first + tile]
        scores = (scores + bias[:, None, :]).reshape(length, tile)
        top = jnp.max(scores, axis=0, keepdims=True)
        expo = jnp.exp((scores - top) * scale)
        prob = expo * (1.0 / jnp.sum(expo, axis=0, keepdims=True))
        prob_b = prob.astype(bf16)
        out_t = dot(val_t, prob_b).astype(bf16)
        delta = jnp.sum(g_t.astype(f32) * out_t.astype(f32), axis=0, keepdims=True)
        dscore = (prob * (dot(val, g_t) - delta)).astype(bf16)
        dquery_t = (dot(key_t, dscore) * scale).astype(bf16)
        give(0, first, out_t.T)
        give(1, first, dquery_t.T)
        dk, dv = dot(dscore, q), dot(prob_b, g)
        dkey = dk if dkey is None else dkey + dk
        dval = dv if dval is None else dval + dv
    give(2, 0, (dkey * scale).astype(bf16))
    give(3, 0, dval.astype(bf16))


def block_bias(rand_blocks, glob_blocks, me, ranks, local_blocks):
    total = ranks * local_blocks
    ids = jnp.arange(total, dtype=jnp.int32)
    order = (me ^ ids // local_blocks) * local_blocks + ids % local_blocks
    rand = jnp.take(rand_blocks, order, axis=0)
    gap = (order[:, None] - order[None, :]) % total
    near = (gap <= 1) | (gap == total - 1)
    glob = jnp.any(order[:, None] == glob_blocks[None, :], axis=1)
    picked = jnp.any(order[:, None, None] == rand[None, :, :], axis=2)
    allowed = near | glob[:, None] | picked
    bias = jnp.where(allowed, 0.0, -jnp.inf).astype(jnp.float32)
    return jnp.repeat(bias, BLOCK, axis=1)


def local(queries, keys, values, grad_out, rand_blocks, glob_blocks):
    ranks = lax.axis_size("ctx")
    me = lax.axis_index("ctx")
    tokens, features = queries.shape[1], queries.shape[2]
    head_dim = features // HEADS
    heads = HEADS // ranks
    me_arr = jnp.reshape(me, (1,)).astype(jnp.int32)
    arrays = [
        pltpu.with_memory_space_constraint(x[0], pltpu.HBM)
        for x in (queries, keys, values, grad_out)
    ]
    piece = pltpu.VMEM((4, tokens, head_dim), jnp.bfloat16)
    full = jax.ShapeDtypeStruct((tokens, features), jnp.bfloat16)

    def on_chip(xs):
        return [pltpu.with_memory_space_constraint(x, pltpu.VMEM) for x in xs]

    def pack(wanted):
        pieces = pl.pallas_call(
            functools.partial(pack_kernel, ranks=ranks, wanted=wanted),
            out_shape=[piece] * len(wanted),
            in_specs=[SMEM] + [ANY] * 4,
            out_specs=[VMEM] * len(wanted),
            scratch_shapes=[pltpu.SemaphoreType.DMA((len(wanted), 4))],
            compiler_params=PARAMS,
        )(me_arr, *arrays)
        return dict(zip(wanted, pieces))

    def permute(x, step):
        return lax.ppermute(x, "ctx", [(j, j ^ step) for j in range(ranks)])

    def attend(got):
        return pl.pallas_call(
            functools.partial(
                attention_kernel, ranks=ranks, tokens=tokens, scale=head_dim ** (-0.5)
            ),
            out_shape=[piece] * ranks,
            in_specs=[VMEM] * (1 + ranks),
            out_specs=[VMEM] * ranks,
            compiler_params=PARAMS,
        )(bias, *on_chip(got))

    slots = [(head, step) for head in range(heads) for step in range(ranks)]
    early = [(0, step) for step in range(1, ranks)]
    pieces = pack(early)
    pieces.update(pack([slot for slot in slots if slot not in early]))
    got = {
        slot: permute(pieces[slot], slot[1]) if slot[1] else pieces[slot] for slot in slots
    }
    bias = block_bias(rand_blocks[0], glob_blocks[0], me, ranks, tokens // BLOCK)
    back = []
    for head in range(heads):
        sent = attend([got[head, step] for step in range(ranks)])
        back += [permute(x, step) if step else x for step, x in enumerate(sent)]
    outs = pl.pallas_call(
        functools.partial(unpack_kernel, ranks=ranks, heads=heads),
        out_shape=[full] * 4,
        in_specs=[SMEM] + [VMEM] * len(back),
        out_specs=[ANY] * 4,
        scratch_shapes=[
            pltpu.VMEM((4, tokens, features), jnp.bfloat16),
            pltpu.SemaphoreType.DMA((4,)),
        ],
        compiler_params=PARAMS,
    )(me_arr, *on_chip(back))
    return tuple(x[None] for x in outs)


def solution(mesh):
    wide = P(("groups", "dp"), "ctx", None)
    return jax.shard_map(
        local,
        mesh=mesh,
        in_specs=(wide,) * 4 + (P(("groups", "dp"), None, None), P(("groups", "dp"), None)),
        out_specs=(wide,) * 4,
        check_vma=False,
    )
```

```python
import functools

import jax
import jax.numpy as jnp
from jax import lax
from jax.experimental import pallas as pl
from jax.experimental.pallas import tpu as pltpu
from jax.sharding import PartitionSpec as P

HEADS = 16
BLOCK = 64
QUERY_TILE = 512
ANY = pl.BlockSpec(memory_space=pl.ANY)
SMEM = pl.BlockSpec(memory_space=pltpu.SMEM)
VMEM = pl.BlockSpec(memory_space=pltpu.VMEM)
PARAMS = pltpu.CompilerParams(vmem_limit_bytes=48 << 20)


def pack_kernel(me_ref, *refs, ranks, wanted):
    arrays, outs, sems = refs[:4], refs[4:-1], refs[-1]
    features, width = arrays[0].shape[1], outs[0].shape[2]
    copies = []
    for n, (head, step) in enumerate(wanted):
        dest = me_ref[0] ^ step
        start = pl.multiple_of(dest * (features // ranks) + head * width, 128)
        for i, array in enumerate(arrays):
            copies.append(
                pltpu.make_async_copy(
                    array.at[:, pl.ds(start, width)], outs[n].at[i], sems.at[n, i]
                )
            )
    for copy in copies:
        copy.start()
    for copy in copies:
        copy.wait()


def unpack_kernel(me_ref, *refs, ranks, heads):
    pieces, outs, buffers, sems = refs[: ranks * heads], refs[ranks * heads : -2], refs[-2], refs[-1]
    features, width = outs[0].shape[1], pieces[0].shape[2]
    copies = []
    for i, out in enumerate(outs):
        for head in range(heads):
            for step in range(ranks):
                dest = me_ref[0] ^ step
                start = pl.multiple_of(dest * (features // ranks) + head * width, 128)
                buffers[i, :, pl.ds(start, width)] = pieces[head * ranks + step][i]
        copies.append(pltpu.make_async_copy(buffers.at[i], out, sems.at[i]))
        copies[-1].start()
    for copy in copies:
        copy.wait()


def attention_kernel(bias_ref, *refs, ranks, tokens, scale):
    got, sent = refs[:ranks], refs[ranks:]
    f32, bf16 = jnp.float32, jnp.bfloat16
    length = ranks * tokens
    tile = min(QUERY_TILE, length)

    def whole(i):
        return jnp.concatenate([piece[i] for piece in got], axis=0)

    def dot(a, b):
        return jnp.dot(a, b, preferred_element_type=f32)

    def give(i, first, value):
        for r in range(value.shape[0] // tokens):
            sent[first // tokens + r][i] = value[r * tokens : (r + 1) * tokens]

    query, key, val, dout = (whole(i) for i in range(4))
    key_t, val_t = key.T, val.T
    dkey = dval = None
    for first in range(0, length, tile):
        q = query[first : first + tile]
        g = dout[first : first + tile]
        g_t = g.T
        scores = dot(key, q.T).reshape(-1, BLOCK, tile)
        bias = bias_ref[:, first : first + tile]
        scores = (scores + bias[:, None, :]).reshape(length, tile)
        top = jnp.max(scores, axis=0, keepdims=True)
        expo = jnp.exp((scores - top) * scale)
        prob = expo * (1.0 / jnp.sum(expo, axis=0, keepdims=True))
        prob_b = prob.astype(bf16)
        out_t = dot(val_t, prob_b).astype(bf16)
        delta = jnp.sum(g_t.astype(f32) * out_t.astype(f32), axis=0, keepdims=True)
        dscore = (prob * (dot(val, g_t) - delta)).astype(bf16)
        dquery_t = (dot(key_t, dscore) * scale).astype(bf16)
        give(0, first, out_t.T)
        give(1, first, dquery_t.T)
        dk, dv = dot(dscore, q), dot(prob_b, g)
        dkey = dk if dkey is None else dkey + dk
        dval = dv if dval is None else dval + dv
    give(2, 0, (dkey * scale).astype(bf16))
    give(3, 0, dval.astype(bf16))


def block_bias(rand_blocks, glob_blocks, me, ranks, local_blocks):
    total = ranks * local_blocks
    ids = jnp.arange(total, dtype=jnp.int32)
    order = (me ^ ids // local_blocks) * local_blocks + ids % local_blocks
    rand = jnp.take(rand_blocks, order, axis=0)
    gap = (order[:, None] - order[None, :]) % total
    near = (gap <= 1) | (gap == total - 1)
    glob = jnp.any(order[:, None] == glob_blocks[None, :], axis=1)
    picked = jnp.any(order[:, None, None] == rand[None, :, :], axis=2)
    allowed = near | glob[:, None] | picked
    bias = jnp.where(allowed, 0.0, -jnp.inf).astype(jnp.float32)
    return jnp.repeat(bias, BLOCK, axis=1)


def local(queries, keys, values, grad_out, rand_blocks, glob_blocks):
    ranks = lax.axis_size("ctx")
    me = lax.axis_index("ctx")
    tokens, features = queries.shape[1], queries.shape[2]
    head_dim = features // HEADS
    heads = HEADS // ranks
    me_arr = jnp.reshape(me, (1,)).astype(jnp.int32)
    arrays = [
        pltpu.with_memory_space_constraint(x[0], pltpu.HBM)
        for x in (queries, keys, values, grad_out)
    ]
    piece = pltpu.VMEM((4, tokens, head_dim), jnp.bfloat16)
    full = jax.ShapeDtypeStruct((tokens, features), jnp.bfloat16)

    def on_chip(xs):
        return [pltpu.with_memory_space_constraint(x, pltpu.VMEM) for x in xs]

    def pack(wanted):
        pieces = pl.pallas_call(
            functools.partial(pack_kernel, ranks=ranks, wanted=wanted),
            out_shape=[piece] * len(wanted),
            in_specs=[SMEM] + [ANY] * 4,
            out_specs=[VMEM] * len(wanted),
            scratch_shapes=[pltpu.SemaphoreType.DMA((len(wanted), 4))],
            compiler_params=PARAMS,
        )(me_arr, *arrays)
        return dict(zip(wanted, pieces))

    def permute(x, step):
        return lax.ppermute(x, "ctx", [(j, j ^ step) for j in range(ranks)])

    def attend(got):
        return pl.pallas_call(
            functools.partial(
                attention_kernel, ranks=ranks, tokens=tokens, scale=head_dim ** (-0.5)
            ),
            out_shape=[piece] * ranks,
            in_specs=[VMEM] * (1 + ranks),
            out_specs=[VMEM] * ranks,
            compiler_params=PARAMS,
        )(bias, *on_chip(got))

    steps = [*range(ranks - 1, -1, -1)]
    slots = [(head, step) for head in range(heads) for step in steps]
    early = [(0, step) for step in steps if step > 1]
    pieces = pack(early)
    pieces.update(pack([slot for slot in slots if slot not in early]))
    got = {
        slot: permute(pieces[slot], slot[1]) if slot[1] else pieces[slot] for slot in slots
    }
    bias = block_bias(rand_blocks[0], glob_blocks[0], me, ranks, tokens // BLOCK)
    back = []
    for head in range(heads):
        sent = attend([got[head, step] for step in range(ranks)])
        moved = {step: permute(sent[step], step) if step else sent[step] for step in steps}
        back += [moved[step] for step in range(ranks)]
    outs = pl.pallas_call(
        functools.partial(unpack_kernel, ranks=ranks, heads=heads),
        out_shape=[full] * 4,
        in_specs=[SMEM] + [VMEM] * len(back),
        out_specs=[ANY] * 4,
        scratch_shapes=[
            pltpu.VMEM((4, tokens, features), jnp.bfloat16),
            pltpu.SemaphoreType.DMA((4,)),
        ],
        compiler_params=PARAMS,
    )(me_arr, *on_chip(back))
    return tuple(x[None] for x in outs)


def solution(mesh):
    wide = P(("groups", "dp"), "ctx", None)
    return jax.shard_map(
        local,
        mesh=mesh,
        in_specs=(wide,) * 4 + (P(("groups", "dp"), None, None), P(("groups", "dp"), None)),
        out_specs=(wide,) * 4,
        check_vma=False,
    )
```

```python
import functools

import jax
import jax.numpy as jnp
from jax import lax
from jax.experimental import pallas as pl
from jax.experimental.pallas import tpu as pltpu
from jax.sharding import PartitionSpec as P

HEADS = 16
BLOCK = 64
QUERY_TILE = 512
ANY = pl.BlockSpec(memory_space=pl.ANY)
SMEM = pl.BlockSpec(memory_space=pltpu.SMEM)
VMEM = pl.BlockSpec(memory_space=pltpu.VMEM)
PARAMS = pltpu.CompilerParams(vmem_limit_bytes=48 << 20)


def pack_kernel(me_ref, *refs, ranks, wanted):
    arrays, outs, sems = refs[:4], refs[4:-1], refs[-1]
    features, width = arrays[0].shape[1], outs[0].shape[2]
    copies = []
    for n, (head, step) in enumerate(wanted):
        dest = me_ref[0] ^ step
        start = pl.multiple_of(dest * (features // ranks) + head * width, 128)
        for i, array in enumerate(arrays):
            copies.append(
                pltpu.make_async_copy(
                    array.at[:, pl.ds(start, width)], outs[n].at[i], sems.at[n, i]
                )
            )
    for copy in copies:
        copy.start()
    for copy in copies:
        copy.wait()


def rows_kernel(me_ref, *refs, ranks, wanted):
    pieces, outs, buffers, sems = refs[: len(wanted)], refs[len(wanted) : -2], refs[-2], refs[-1]
    features, width = outs[0].shape[1], pieces[0].shape[2]
    copies = []
    for i, out in enumerate(outs):
        for n, (head, step) in enumerate(wanted):
            dest = me_ref[0] ^ step
            start = pl.multiple_of(dest * (features // ranks) + head * width, 128)
            buffers[i, :, pl.ds(start, width)] = pieces[n][i]
        copies.append(pltpu.make_async_copy(buffers.at[i], out, sems.at[i]))
        copies[-1].start()
    for copy in copies:
        copy.wait()


def columns_kernel(me_ref, *refs, ranks, wanted):
    pieces, outs, sems = refs[: len(wanted)], refs[-5:-1], refs[-1]
    features, width = outs[0].shape[1], pieces[0].shape[2]
    copies = []
    for n, (head, step) in enumerate(wanted):
        dest = me_ref[0] ^ step
        start = pl.multiple_of(dest * (features // ranks) + head * width, 128)
        for i, out in enumerate(outs):
            copies.append(
                pltpu.make_async_copy(
                    pieces[n].at[i], out.at[:, pl.ds(start, width)], sems.at[n, i]
                )
            )
    for copy in copies:
        copy.start()
    for copy in copies:
        copy.wait()


def attention_kernel(bias_ref, *refs, ranks, tokens, scale, order):
    got, sent = [refs[order.index(step)] for step in range(ranks)], refs[ranks:]
    f32, bf16 = jnp.float32, jnp.bfloat16
    length = ranks * tokens
    tile = min(QUERY_TILE, length)

    def whole(i):
        return jnp.concatenate([piece[i] for piece in got], axis=0)

    def dot(a, b):
        return jnp.dot(a, b, preferred_element_type=f32)

    def give(i, first, value):
        for r in range(value.shape[0] // tokens):
            sent[first // tokens + r][i] = value[r * tokens : (r + 1) * tokens]

    query, key, val, dout = (whole(i) for i in range(4))
    key_t, val_t = key.T, val.T
    dkey = dval = None
    for first in range(0, length, tile):
        q = query[first : first + tile]
        g = dout[first : first + tile]
        g_t = g.T
        scores = dot(key, q.T).reshape(-1, BLOCK, tile)
        bias = bias_ref[:, first : first + tile]
        scores = (scores + bias[:, None, :]).reshape(length, tile)
        top = jnp.max(scores, axis=0, keepdims=True)
        expo = jnp.exp((scores - top) * scale)
        prob = expo * (1.0 / jnp.sum(expo, axis=0, keepdims=True))
        prob_b = prob.astype(bf16)
        out_t = dot(val_t, prob_b).astype(bf16)
        delta = jnp.sum(g_t.astype(f32) * out_t.astype(f32), axis=0, keepdims=True)
        dscore = (prob * (dot(val, g_t) - delta)).astype(bf16)
        dquery_t = (dot(key_t, dscore) * scale).astype(bf16)
        give(0, first, out_t.T)
        give(1, first, dquery_t.T)
        dk, dv = dot(dscore, q), dot(prob_b, g)
        dkey = dk if dkey is None else dkey + dk
        dval = dv if dval is None else dval + dv
    give(2, 0, (dkey * scale).astype(bf16))
    give(3, 0, dval.astype(bf16))


def block_bias(rand_blocks, glob_blocks, me, ranks, local_blocks):
    total = ranks * local_blocks
    ids = jnp.arange(total, dtype=jnp.int32)
    order = (me ^ ids // local_blocks) * local_blocks + ids % local_blocks
    rand = jnp.take(rand_blocks, order, axis=0)
    gap = (order[:, None] - order[None, :]) % total
    near = (gap <= 1) | (gap == total - 1)
    glob = jnp.any(order[:, None] == glob_blocks[None, :], axis=1)
    picked = jnp.any(order[:, None, None] == rand[None, :, :], axis=2)
    allowed = near | glob[:, None] | picked
    bias = jnp.where(allowed, 0.0, -jnp.inf).astype(jnp.float32)
    return jnp.repeat(bias, BLOCK, axis=1)


def local(queries, keys, values, grad_out, rand_blocks, glob_blocks):
    ranks = lax.axis_size("ctx")
    me = lax.axis_index("ctx")
    tokens, features = queries.shape[1], queries.shape[2]
    head_dim = features // HEADS
    heads = HEADS // ranks
    me_arr = jnp.reshape(me, (1,)).astype(jnp.int32)
    arrays = [
        pltpu.with_memory_space_constraint(x[0], pltpu.HBM)
        for x in (queries, keys, values, grad_out)
    ]
    piece = pltpu.VMEM((4, tokens, head_dim), jnp.bfloat16)
    full = jax.ShapeDtypeStruct((tokens, features), jnp.bfloat16)

    def on_chip(xs):
        return [pltpu.with_memory_space_constraint(x, pltpu.VMEM) for x in xs]

    def pack(wanted):
        pieces = pl.pallas_call(
            functools.partial(pack_kernel, ranks=ranks, wanted=wanted),
            out_shape=[piece] * len(wanted),
            in_specs=[SMEM] + [ANY] * 4,
            out_specs=[VMEM] * len(wanted),
            scratch_shapes=[pltpu.SemaphoreType.DMA((len(wanted), 4))],
            compiler_params=PARAMS,
        )(me_arr, *arrays)
        return dict(zip(wanted, pieces))

    def permute(x, step):
        return lax.ppermute(x, "ctx", [(j, j ^ step) for j in range(ranks)])

    def attend(got, order):
        return pl.pallas_call(
            functools.partial(
                attention_kernel, ranks=ranks, tokens=tokens, scale=head_dim ** (-0.5), order=order
            ),
            out_shape=[piece] * ranks,
            in_specs=[VMEM] * (1 + ranks),
            out_specs=[VMEM] * ranks,
            compiler_params=PARAMS,
        )(bias, *on_chip(got))

    steps = [*range(ranks - 1, -1, -1)]
    orders = [[0, 1, *range(ranks - 1, 1, -1)]] + [[*range(2, ranks), 1, 0]] * (heads - 1)
    order_out = [*range(2, ranks), 1, 0]
    slots = [(head, step) for head in range(heads) for step in steps]
    early = [(0, step) for step in steps if step > 1]
    pieces = pack(early)
    pieces.update(pack([slot for slot in slots if slot not in early]))
    got = {
        slot: permute(pieces[slot], slot[1]) if slot[1] else pieces[slot] for slot in slots
    }
    bias = block_bias(rand_blocks[0], glob_blocks[0], me, ranks, tokens // BLOCK)
    back = []
    for head in range(heads):
        sent = attend([got[head, step] for step in orders[head]], orders[head])
        moved = {step: permute(sent[step], step) if step else sent[step] for step in steps}
        back += [moved[step] for step in order_out]

    def unpack(kernel, wanted, scratch, outs):
        return pl.pallas_call(
            functools.partial(kernel, ranks=ranks, wanted=wanted),
            out_shape=[full] * 4,
            in_specs=[SMEM] + [VMEM] * len(wanted) + [ANY] * len(outs),
            out_specs=[ANY] * 4,
            scratch_shapes=scratch,
            input_output_aliases={1 + len(wanted) + i: i for i in range(len(outs))},
            compiler_params=PARAMS,
        )(me_arr, *on_chip([back[h * ranks + order_out.index(s)] for h, s in wanted]), *outs)

    rows = [
        pltpu.VMEM((4, tokens, features), jnp.bfloat16),
        pltpu.SemaphoreType.DMA((4,)),
    ]
    done = [(head, step) for head in range(heads) for step in order_out]
    last = [slot for slot in done if slot[0] == heads - 1 and slot[1]]
    outs = []
    if len(last) < len(done):
        outs = unpack(rows_kernel, [slot for slot in done if slot not in last], rows, outs)
    outs = unpack(columns_kernel, last, [pltpu.SemaphoreType.DMA((len(last), 4))], outs)
    return tuple(x[None] for x in outs)


def solution(mesh):
    wide = P(("groups", "dp"), "ctx", None)
    return jax.shard_map(
        local,
        mesh=mesh,
        in_specs=(wide,) * 4 + (P(("groups", "dp"), None, None), P(("groups", "dp"), None)),
        out_specs=(wide,) * 4,
        check_vma=False,
    )
```

```python
import functools

import jax
import jax.numpy as jnp
from jax import lax
from jax.experimental import pallas as pl
from jax.experimental.pallas import tpu as pltpu
from jax.sharding import PartitionSpec as P

HEADS = 16
BLOCK = 64
QUERY_TILE = 512
ANY = pl.BlockSpec(memory_space=pl.ANY)
SMEM = pl.BlockSpec(memory_space=pltpu.SMEM)
VMEM = pl.BlockSpec(memory_space=pltpu.VMEM)
PARAMS = pltpu.CompilerParams(vmem_limit_bytes=48 << 20)


def pack_kernel(me_ref, *refs, ranks, wanted):
    arrays, outs, sems = refs[:4], refs[4:-1], refs[-1]
    features, width = arrays[0].shape[1], outs[0].shape[2]
    copies = []
    for n, (head, step) in enumerate(wanted):
        dest = me_ref[0] ^ step
        start = pl.multiple_of(dest * (features // ranks) + head * width, 128)
        for i, array in enumerate(arrays):
            copies.append(
                pltpu.make_async_copy(
                    array.at[:, pl.ds(start, width)], outs[n].at[i], sems.at[n, i]
                )
            )
    for copy in copies:
        copy.start()
    for copy in copies:
        copy.wait()


def rows_kernel(me_ref, *refs, ranks, wanted):
    pieces, outs, buffers, sems = refs[: len(wanted)], refs[len(wanted) : -2], refs[-2], refs[-1]
    features, width = outs[0].shape[1], pieces[0].shape[2]
    copies = []
    for i, out in enumerate(outs):
        for n, (head, step) in enumerate(wanted):
            dest = me_ref[0] ^ step
            start = pl.multiple_of(dest * (features // ranks) + head * width, 128)
            buffers[i, :, pl.ds(start, width)] = pieces[n][i]
        copies.append(pltpu.make_async_copy(buffers.at[i], out, sems.at[i]))
        copies[-1].start()
    for copy in copies:
        copy.wait()


def columns_kernel(me_ref, *refs, ranks, wanted):
    pieces, outs, sems = refs[: len(wanted)], refs[-5:-1], refs[-1]
    features, width = outs[0].shape[1], pieces[0].shape[2]
    copies = []
    for n, (head, step) in enumerate(wanted):
        dest = me_ref[0] ^ step
        start = pl.multiple_of(dest * (features // ranks) + head * width, 128)
        for i, out in enumerate(outs):
            copies.append(
                pltpu.make_async_copy(
                    pieces[n].at[i], out.at[:, pl.ds(start, width)], sems.at[n, i]
                )
            )
    for copy in copies:
        copy.start()
    for copy in copies:
        copy.wait()


def attention_kernel(bias_ref, *refs, ranks, tokens, scale, order):
    got, sent = [refs[order.index(step)] for step in range(ranks)], refs[ranks:]
    f32, bf16 = jnp.float32, jnp.bfloat16
    length = ranks * tokens
    tile = min(QUERY_TILE, length)

    def whole(i):
        return jnp.concatenate([piece[i] for piece in got], axis=0)

    def dot(a, b):
        return jnp.dot(a, b, preferred_element_type=f32)

    def give(i, first, value):
        for r in range(value.shape[0] // tokens):
            sent[first // tokens + r][i] = value[r * tokens : (r + 1) * tokens]

    query, key, val, dout = (whole(i) for i in range(4))
    key_t, val_t = key.T, val.T
    dkey = dval = None
    for first in range(0, length, tile):
        q = query[first : first + tile]
        g = dout[first : first + tile]
        g_t = g.T
        scores = dot(key, q.T).reshape(-1, BLOCK, tile)
        bias = bias_ref[:, first : first + tile]
        scores = (scores + bias[:, None, :]).reshape(length, tile)
        top = jnp.max(scores, axis=0, keepdims=True)
        expo = jnp.exp((scores - top) * scale)
        prob = expo * (1.0 / jnp.sum(expo, axis=0, keepdims=True))
        prob_b = prob.astype(bf16)
        out_t = dot(val_t, prob_b).astype(bf16)
        delta = jnp.sum(g_t.astype(f32) * out_t.astype(f32), axis=0, keepdims=True)
        dscore = (prob * (dot(val, g_t) - delta)).astype(bf16)
        dquery_t = (dot(key_t, dscore) * scale).astype(bf16)
        give(0, first, out_t.T)
        give(1, first, dquery_t.T)
        dk, dv = dot(dscore, q), dot(prob_b, g)
        dkey = dk if dkey is None else dkey + dk
        dval = dv if dval is None else dval + dv
    give(2, 0, (dkey * scale).astype(bf16))
    give(3, 0, dval.astype(bf16))


def block_bias(rand_blocks, glob_blocks, me, ranks, local_blocks):
    total = ranks * local_blocks
    ids = jnp.arange(total, dtype=jnp.int32)
    order = (me ^ ids // local_blocks) * local_blocks + ids % local_blocks
    rand = jnp.take(rand_blocks, order, axis=0)
    gap = (order[:, None] - order[None, :]) % total
    near = (gap <= 1) | (gap == total - 1)
    glob = jnp.any(order[:, None] == glob_blocks[None, :], axis=1)
    picked = jnp.any(order[:, None, None] == rand[None, :, :], axis=2)
    allowed = near | glob[:, None] | picked
    bias = jnp.where(allowed, 0.0, -jnp.inf).astype(jnp.float32)
    return jnp.repeat(bias, BLOCK, axis=1)


def local(queries, keys, values, grad_out, rand_blocks, glob_blocks):
    ranks = lax.axis_size("ctx")
    me = lax.axis_index("ctx")
    tokens, features = queries.shape[1], queries.shape[2]
    head_dim = features // HEADS
    heads = HEADS // ranks
    me_arr = jnp.reshape(me, (1,)).astype(jnp.int32)
    arrays = [
        pltpu.with_memory_space_constraint(x[0], pltpu.HBM)
        for x in (queries, keys, values, grad_out)
    ]
    piece = pltpu.VMEM((4, tokens, head_dim), jnp.bfloat16)
    full = jax.ShapeDtypeStruct((tokens, features), jnp.bfloat16)

    def on_chip(xs):
        return [pltpu.with_memory_space_constraint(x, pltpu.VMEM) for x in xs]

    def pack(wanted):
        pieces = pl.pallas_call(
            functools.partial(pack_kernel, ranks=ranks, wanted=wanted),
            out_shape=[piece] * len(wanted),
            in_specs=[SMEM] + [ANY] * 4,
            out_specs=[VMEM] * len(wanted),
            scratch_shapes=[pltpu.SemaphoreType.DMA((len(wanted), 4))],
            compiler_params=PARAMS,
        )(me_arr, *arrays)
        return dict(zip(wanted, pieces))

    def permute(x, step):
        return lax.ppermute(x, "ctx", [(j, j ^ step) for j in range(ranks)])

    def attend(got, order):
        return pl.pallas_call(
            functools.partial(
                attention_kernel, ranks=ranks, tokens=tokens, scale=head_dim ** (-0.5), order=order
            ),
            out_shape=[piece] * ranks,
            in_specs=[VMEM] * (1 + ranks),
            out_specs=[VMEM] * ranks,
            compiler_params=PARAMS,
        )(bias, *on_chip(got))

    steps = [*range(ranks - 1, -1, -1)]
    orders = [[0, 1, *range(ranks - 1, 1, -1)]] + [[*range(2, ranks), 1, 0]] * (heads - 1)
    order_out = [*range(2, ranks), 1, 0]
    slots = [(head, step) for head in range(heads) for step in steps]
    early = [(0, step) for step in steps if step > 1]
    pieces = {}
    for wanted in (early[:1], early[1:], [slot for slot in slots if slot not in early]):
        if wanted:
            pieces.update(pack(wanted))
    got = {
        slot: permute(pieces[slot], slot[1]) if slot[1] else pieces[slot] for slot in slots
    }
    bias = block_bias(rand_blocks[0], glob_blocks[0], me, ranks, tokens // BLOCK)
    back = []
    for head in range(heads):
        sent = attend([got[head, step] for step in orders[head]], orders[head])
        moved = {step: permute(sent[step], step) if step else sent[step] for step in steps}
        back += [moved[step] for step in order_out]

    def unpack(kernel, wanted, scratch, outs):
        return pl.pallas_call(
            functools.partial(kernel, ranks=ranks, wanted=wanted),
            out_shape=[full] * 4,
            in_specs=[SMEM] + [VMEM] * len(wanted) + [ANY] * len(outs),
            out_specs=[ANY] * 4,
            scratch_shapes=scratch,
            input_output_aliases={1 + len(wanted) + i: i for i in range(len(outs))},
            compiler_params=PARAMS,
        )(me_arr, *on_chip([back[h * ranks + order_out.index(s)] for h, s in wanted]), *outs)

    rows = [
        pltpu.VMEM((4, tokens, features), jnp.bfloat16),
        pltpu.SemaphoreType.DMA((4,)),
    ]
    done = [(head, step) for head in range(heads) for step in order_out]
    last = [slot for slot in done if slot[0] == heads - 1 and slot[1] >= min(2, ranks - 1)]
    outs = []
    if len(last) < len(done):
        outs = unpack(rows_kernel, [slot for slot in done if slot not in last], rows, outs)
    outs = unpack(columns_kernel, last, [pltpu.SemaphoreType.DMA((len(last), 4))], outs)
    return tuple(x[None] for x in outs)


def solution(mesh):
    wide = P(("groups", "dp"), "ctx", None)
    return jax.shard_map(
        local,
        mesh=mesh,
        in_specs=(wide,) * 4 + (P(("groups", "dp"), None, None), P(("groups", "dp"), None)),
        out_specs=(wide,) * 4,
        check_vma=False,
    )
```
